32 devices in a mesh: dp: 8 (over z, core), tensor: 4 (over y, x).
Axes of the slice: x: 2, y: 2, z: 4, core: 2. Of those that a mesh axis runs over, the one named last changes fastest.
Arguments:
- tokens: bfloat16 [8192, 1024], P('dp'), may hold values from -6 to 6
- segment_ids: int32 [8, 1024], P('dp'), may hold values from 0 to 7, never falling along the last dimension, each value on 1 to 512 neighbouring positions
- ln1_gain: float32 [1024], replicated, may hold values from 0.1 to 1.9
- ln1_shift: float32 [1024], replicated, may hold values from -1.75 to 1.75
- w_qkv: bfloat16 [3, 1024, 1024], P(None, None, 'tensor'), may hold values from -2 to 2
- b_qv: float32 [2, 1024], P(None, 'tensor'), may hold values from -3 to 3
- w_out: bfloat16 [1024, 1024], P('tensor'), may hold values from -0.75 to 0.75
- b_out: float32 [1024], replicated, may hold values from -3 to 3
- ln2_gain: float32 [1024], replicated, may hold values from 0.1 to 1.9
- ln2_shift: float32 [1024], replicated, may hold values from -1.75 to 1.75
- w_up: bfloat16 [1024, 4096], P(None, 'tensor'), may hold values from -0.1875 to 0.1875
- b_up: float32 [4096], P('tensor'), may hold values from -3 to 3
- w_down: bfloat16 [4096, 1024], P('tensor'), may hold values from -0.09375 to 0.09375
- b_down: float32 [1024], replicated, may hold values from -3 to 3
- d_out: bfloat16 [8192, 1024], P('dp'), may hold values from -6 to 6
Outputs:
- output: bfloat16 [8192, 1024], P('dp')
- d_tokens: bfloat16 [8192, 1024], P('dp')
- g_ln1_gain: float32 [1024], replicated
- g_ln1_shift: float32 [1024], replicated
- g_qkv: float32 [3, 1024, 1024], P(None, None, 'tensor')
- g_qv_bias: float32 [2, 1024], P(None, 'tensor')
- g_out: float32 [1024, 1024], P('tensor')
- g_out_bias: float32 [1024], replicated
- g_ln2_gain: float32 [1024], replicated
- g_ln2_shift: float32 [1024], replicated
- g_up: float32 [1024, 4096], P(None, 'tensor')
- g_up_bias: float32 [4096], P('tensor')
- g_down: float32 [4096, 1024], P('tensor')
- g_down_bias: float32 [1024], replicated
The draws below stay inside these ranges and needn't reach their ends.
Inputs may be any that keep to these rules, and one draw needn't show every extreme that they name: `segment_ids`: each row numbers its packed sequences from 0 without falling; every sequence has 1 to 512 tokens and one has exactly 512.
All inputs are finite; a program needn't handle non-finite values.
Results may differ from the reference program's by a relative error of at most 0.019.
Values may be sent and summed in bfloat16 or wider, within the bound.
A program may use at most 192 MiB of HBM per device.

```python
import math
import jax
import jax.numpy as jnp
import numpy as np
from jax import lax

D = 1024
H = 16
FF = 4096
TOK_DEV = 1024
HD = 64
SEGS = 8
LONGEST = 512
SHARDS = 8
TOKENS = 8192
N_DP = 8
N_TENSOR = 4


def draw_w_qkv(key, part):
    drawn_values = jnp.clip(jax.random.normal(key, (3, D, D), jnp.float32), -3.0, 3.0) * D ** (-0.5)
    return drawn_values.astype(jnp.bfloat16)


def block_levels(stream_key, dims, shards, smallest, top_value):
    def one(dim, blocks):
        draws = jax.random.uniform(jax.random.fold_in(jax.random.fold_in(stream_key, 6), dim), (blocks,), jnp.float32, smallest / len(shards), top_value / len(shards))
        return jnp.repeat(jnp.exp(draws), dims[dim] // blocks).reshape((-1,) + (1,) * (len(dims) - dim - 1))

    factor_of = one(*shards[0])
    for cut in shards[1:]:
        factor_of = factor_of * one(*cut)
    return factor_of


def profile(number_of, total, most, skew):
    portions = [(1 << 20) // math.isqrt(grade ** skew) + 1 for grade in range(2, number_of + 1)]
    surplus, holding = total - most - (number_of - 1), [1] * (number_of - 1)
    while surplus > 0:
        free = [i for i in range(number_of - 1) if holding[i] < most]
        pool, budget = sum([portions[i] for i in free]), surplus
        for i in free:
            more = min(most - holding[i], max(1, budget * portions[i] // pool), surplus)
            holding[i] = holding[i] + more
            surplus = surplus - more
    return np.array([most] + holding)


def uneven(stream_key, number_of, total, reach, skew):
    if number_of == 2:
        one = jax.random.randint(stream_key, (), max(1, total - reach), min(reach, total - 1) + 1)
        return jnp.stack([one, total - one])
    tallies = jnp.asarray(profile(number_of, total, reach, skew), jnp.int32)
    twos = (number_of - 1) // 2
    giver, sink = tallies[1:1 + 2 * twos:2], tallies[2:2 + 2 * twos:2]
    margin = jnp.minimum(giver - 1, reach - sink)
    moved = jax.random.randint(jax.random.fold_in(stream_key, 1), (twos,), 0, 1 << 20) % (margin + 1)
    tallies = tallies.at[1:1 + 2 * twos:2].set(giver - moved).at[2:2 + 2 * twos:2].set(sink + moved)
    return tallies[jax.random.permutation(jax.random.fold_in(stream_key, 2), number_of)]


def centred(own_key, extent, scale, most, split=(), held_as=jnp.bfloat16):
    array = jax.random.normal(own_key, extent, jnp.float32) * scale
    if len(split) > 0:
        array = block_levels(own_key, extent, split, -0.22, 0.18) * array
    return jnp.clip(array, min=-most, max=most).astype(held_as)


def setup_inputs(seed: int = 0) -> dict:
    arg_keys = jax.random.split(jax.random.key(seed), 16)
    return {
        "tokens": centred(arg_keys[0], (TOKENS, D), 1.0, 6.0, ((0, 8),)),
        "segment_ids": jax.vmap(lambda own: jnp.searchsorted(jnp.cumsum(uneven(own, SEGS, TOK_DEV, LONGEST, 2)), jnp.arange(TOK_DEV), side="right"))(jax.random.split(arg_keys[1], SHARDS)).reshape((SHARDS, TOK_DEV)).astype(jnp.int32),
        "ln1_gain": jnp.clip(1.0 + 0.18 * jax.random.normal(arg_keys[2], (D,), jnp.float32), 0.1, 1.9),
        "ln1_shift": centred(arg_keys[3], (D,), 0.3, 1.75, (), jnp.float32),
        "w_qkv": draw_w_qkv(jax.random.fold_in(arg_keys[15], 71), 0),
        "b_qv": centred(arg_keys[5], (2, D), 0.5, 3.0, ((1, 4),), jnp.float32),
        "w_out": centred(arg_keys[6], (D, D), (D // 16) ** -0.5, 0.75, ((0, 4),)),
        "b_out": centred(arg_keys[7], (D,), 0.5, 3.0, (), jnp.float32),
        "ln2_gain": jnp.clip(1.0 + 0.18 * jax.random.normal(arg_keys[8], (D,), jnp.float32), 0.1, 1.9),
        "ln2_shift": centred(arg_keys[9], (D,), 0.3, 1.75, (), jnp.float32),
        "w_up": centred(arg_keys[10], (D, FF), D ** -0.5, 0.1875, ((1, 4),)),
        "b_up": centred(arg_keys[11], (FF,), 0.5, 3.0, ((0, 4),), jnp.float32),
        "w_down": centred(arg_keys[12], (FF, D), FF ** -0.5, 0.09375, ((0, 4),)),
        "b_down": centred(arg_keys[13], (D,), 0.5, 3.0, (), jnp.float32),
        "d_out": centred(arg_keys[14], (TOKENS, D), 1.0, 6.0, ((0, 8),)),
    }


epsilon = 1e-05
gelu_coef = 0.7978845608028654

def gelu_value(values):
    inner = jnp.tanh(gelu_coef * (values + 0.044715 * values * values * values))
    return 0.5 * values * (1.0 + inner)

def gelu_slope(values):
    inner = jnp.tanh(gelu_coef * (values + 0.044715 * values * values * values))
    return 0.5 * (1.0 + inner) + 0.5 * values * (1.0 - inner * inner) * gelu_coef * (1.0 + 3.0 * 0.044715 * values * values)

def norm_parts(values):
    centered = values - lax.optimization_barrier(jnp.mean(values, axis=-1, keepdims=True))
    inverse = lax.rsqrt(lax.optimization_barrier(jnp.mean(centered * centered, axis=-1, keepdims=True)) + epsilon)
    return (centered * inverse, inverse)

def norm_back(grad_in, normed, inverse, gain):
    scaled = grad_in * gain
    return inverse * (scaled - lax.optimization_barrier(jnp.mean(scaled, axis=-1, keepdims=True)) - normed * lax.optimization_barrier(jnp.mean(scaled * normed, axis=-1, keepdims=True)))

def block_mask(seg_query, seg_keys, first_row):
    shape_here = (seg_query.shape[0], seg_keys.shape[0])
    query_pos = first_row + lax.broadcasted_iota(jnp.int32, shape_here, 0)
    key_pos = lax.broadcasted_iota(jnp.int32, shape_here, 1)
    return (seg_query[:, None] == seg_keys[None, :]) & (key_pos <= query_pos)

def group_round(parts):
    rounded = lax.optimization_barrier(parts.astype(jnp.bfloat16))
    return lax.optimization_barrier(jnp.sum(rounded.astype(jnp.float32), axis=0))

def attention_forward(query_heads, key_heads, value_heads, seg_row):
    length = query_heads.shape[1]
    block_rows = 512 if length >= 512 else length
    scale = query_heads.shape[2] ** (-0.5)
    key_float = key_heads.astype(jnp.float32)
    value_float = value_heads.astype(jnp.float32)
    outputs = []
    totals = []
    for first_row in range(0, length, block_rows):
        rows_q = query_heads[:, first_row:first_row + block_rows].astype(jnp.float32)
        scores = jnp.einsum('hqd,hkd->hqk', rows_q, key_float) * scale
        allowed = block_mask(seg_row[first_row:first_row + block_rows], seg_row, first_row)
        scores = jnp.where(allowed[None], scores, -jnp.inf)
        maximum = lax.optimization_barrier(jnp.max(scores, axis=-1, keepdims=True))
        log_total = jnp.log(lax.optimization_barrier(jnp.sum(jnp.exp(scores - maximum), axis=-1, keepdims=True))) + maximum
        weights_bf = jnp.exp(scores - log_total).astype(jnp.bfloat16)
        outputs.append(jnp.einsum('hqk,hkd->hqd', weights_bf.astype(jnp.float32), value_float).astype(jnp.bfloat16))
        totals.append(log_total)
    return (jnp.concatenate(outputs, axis=1), jnp.concatenate(totals, axis=1))

def attention_backward(query_heads, key_heads, value_heads, seg_row, log_totals, grad_ctx):
    length = query_heads.shape[1]
    block_rows = 512 if length >= 512 else length
    scale = query_heads.shape[2] ** (-0.5)
    key_float = key_heads.astype(jnp.float32)
    value_float = value_heads.astype(jnp.float32)
    grad_keys = jnp.zeros(key_heads.shape, jnp.float32)
    grad_values = jnp.zeros(value_heads.shape, jnp.float32)
    grad_queries = []
    for first_row in range(0, length, block_rows):
        rows_q = query_heads[:, first_row:first_row + block_rows].astype(jnp.float32)
        scores = jnp.einsum('hqd,hkd->hqk', rows_q, key_float) * scale
        allowed = block_mask(seg_row[first_row:first_row + block_rows], seg_row, first_row)
        scores = jnp.where(allowed[None], scores, -jnp.inf)
        weights = jnp.exp(scores - log_totals[:, first_row:first_row + block_rows])
        weights_bf = weights.astype(jnp.bfloat16).astype(jnp.float32)
        grad_rows_ctx = grad_ctx[:, first_row:first_row + block_rows].astype(jnp.float32)
        grad_weights = jnp.einsum('hqd,hkd->hqk', grad_rows_ctx, value_float)
        inner_sum = lax.optimization_barrier(jnp.sum(weights * grad_weights, axis=-1, keepdims=True))
        grad_scores = (weights * (grad_weights - inner_sum)).astype(jnp.bfloat16).astype(jnp.float32)
        grad_queries.append((jnp.einsum('hqk,hkd->hqd', grad_scores, key_float) * scale).astype(jnp.bfloat16))
        grad_keys = grad_keys + jnp.einsum('hqk,hqd->hkd', grad_scores, rows_q) * scale
        grad_values = grad_values + jnp.einsum('hqk,hqd->hkd', weights_bf, grad_rows_ctx)
    return (jnp.concatenate(grad_queries, axis=1), grad_keys.astype(jnp.bfloat16), grad_values.astype(jnp.bfloat16))

def one_shard(tokens, seg_row, d_out, params):
    ln1_gain, ln1_shift, w_qkv, b_qv, w_out, b_out, ln2_gain, ln2_shift, w_up, b_up, w_down, b_down = params
    groups = N_TENSOR
    length = tokens.shape[0]
    width = tokens.shape[1]
    hidden = w_up.shape[1]
    local_width = width // groups
    local_hidden = hidden // groups
    tokens_f = tokens.astype(jnp.float32)
    normed1, inverse1 = norm_parts(tokens_f)
    input1 = (normed1 * ln1_gain + ln1_shift).astype(jnp.bfloat16)
    projected = jnp.einsum('sd,ide->ise', input1.astype(jnp.float32), w_qkv.astype(jnp.float32))
    bias_rows = jnp.stack([b_qv[0], jnp.zeros_like(b_qv[0]), b_qv[1]])
    projected = (projected + bias_rows[:, None, :]).astype(jnp.bfloat16)
    split_heads = projected.reshape(3, length, H, HD).transpose(0, 2, 1, 3)
    query_heads, key_heads, value_heads = (split_heads[0], split_heads[1], split_heads[2])
    context_heads, log_totals = attention_forward(query_heads, key_heads, value_heads, seg_row)
    context = context_heads.transpose(1, 0, 2).reshape(length, width)
    attn_parts = jnp.einsum('sgk,gkd->gsd', context.reshape(length, groups, local_width).astype(jnp.float32), w_out.reshape(groups, local_width, width).astype(jnp.float32))
    resid_mid = tokens_f + group_round(attn_parts) + b_out
    normed2, inverse2 = norm_parts(resid_mid)
    input2 = (normed2 * ln2_gain + ln2_shift).astype(jnp.bfloat16)
    pre_act = jnp.dot(input2, w_up, preferred_element_type=jnp.float32) + b_up
    activated = gelu_value(pre_act).astype(jnp.bfloat16)
    mlp_parts = jnp.einsum('sgk,gkd->gsd', activated.reshape(length, groups, local_hidden).astype(jnp.float32), w_down.reshape(groups, local_hidden, width).astype(jnp.float32))
    output = (resid_mid + group_round(mlp_parts) + b_down).astype(jnp.bfloat16)
    grad_out = d_out.astype(jnp.float32)
    g_down_bias = lax.optimization_barrier(jnp.sum(grad_out, axis=0))
    g_down = jnp.einsum('sf,sd->fd', activated.astype(jnp.float32), grad_out)
    grad_act = jnp.einsum('sd,fd->sf', grad_out, w_down.astype(jnp.float32))
    grad_pre = (grad_act * gelu_slope(pre_act)).astype(jnp.bfloat16)
    g_up = jnp.einsum('sd,sf->df', input2.astype(jnp.float32), grad_pre.astype(jnp.float32))
    g_up_bias = lax.optimization_barrier(jnp.sum(grad_pre.astype(jnp.float32), axis=0))
    normed_parts_grad = jnp.einsum('sgk,dgk->gsd', grad_pre.reshape(length, groups, local_hidden).astype(jnp.float32), w_up.reshape(width, groups, local_hidden).astype(jnp.float32))
    normed_grad = group_round(normed_parts_grad)
    g_ln2_gain = lax.optimization_barrier(jnp.sum(normed_grad * normed2, axis=0))
    g_ln2_shift = lax.optimization_barrier(jnp.sum(normed_grad, axis=0))
    resid_grad = grad_out + norm_back(normed_grad, normed2, inverse2, ln2_gain)
    g_out_bias = lax.optimization_barrier(jnp.sum(resid_grad, axis=0))
    resid_grad_bf = resid_grad.astype(jnp.bfloat16).astype(jnp.float32)
    g_out = jnp.einsum('sk,sd->kd', context.astype(jnp.float32), resid_grad_bf)
    grad_context = jnp.einsum('sd,kd->sk', resid_grad_bf, w_out.astype(jnp.float32)).astype(jnp.bfloat16)
    grad_ctx_heads = grad_context.reshape(length, H, HD).transpose(1, 0, 2)
    grad_q, grad_k, grad_v = attention_backward(query_heads, key_heads, value_heads, seg_row, log_totals, grad_ctx_heads)
    grad_proj = jnp.stack([grad_q, grad_k, grad_v]).transpose(0, 2, 1, 3).reshape(3, length, width)
    grad_proj_f = grad_proj.astype(jnp.float32)
    g_qkv = jnp.einsum('sd,ise->ide', input1.astype(jnp.float32), grad_proj_f)
    g_qv_bias = jnp.stack([lax.optimization_barrier(jnp.sum(grad_proj_f[0], axis=0)), lax.optimization_barrier(jnp.sum(grad_proj_f[2], axis=0))])
    input_parts = jnp.einsum('isgk,idgk->gsd', grad_proj_f.reshape(3, length, groups, local_width), w_qkv.reshape(3, width, groups, local_width).astype(jnp.float32))
    input_grad = group_round(input_parts)
    g_ln1_gain = lax.optimization_barrier(jnp.sum(input_grad * normed1, axis=0))
    g_ln1_shift = lax.optimization_barrier(jnp.sum(input_grad, axis=0))
    d_tokens = (resid_grad + norm_back(input_grad, normed1, inverse1, ln1_gain)).astype(jnp.bfloat16)
    grads = (g_ln1_gain, g_ln1_shift, g_qkv, g_qv_bias, g_out, g_out_bias, g_ln2_gain, g_ln2_shift, g_up, g_up_bias, g_down, g_down_bias)
    return (output, d_tokens, grads)

def reference(tokens, segment_ids, ln1_gain, ln1_shift, w_qkv, b_qv, w_out, b_out, ln2_gain, ln2_shift, w_up, b_up, w_down, b_down, d_out):
    params = (ln1_gain, ln1_shift, w_qkv, b_qv, w_out, b_out, ln2_gain, ln2_shift, w_up, b_up, w_down, b_down)
    width = tokens.shape[1]
    token_blocks = tokens.reshape(N_DP, TOK_DEV, width)
    grad_blocks = d_out.reshape(N_DP, TOK_DEV, width)
    zero_grads = (jnp.zeros(ln1_gain.shape, jnp.float32), jnp.zeros(ln1_shift.shape, jnp.float32), jnp.zeros(w_qkv.shape, jnp.float32), jnp.zeros(b_qv.shape, jnp.float32), jnp.zeros(w_out.shape, jnp.float32), jnp.zeros(b_out.shape, jnp.float32), jnp.zeros(ln2_gain.shape, jnp.float32), jnp.zeros(ln2_shift.shape, jnp.float32), jnp.zeros(w_up.shape, jnp.float32), jnp.zeros(b_up.shape, jnp.float32), jnp.zeros(w_down.shape, jnp.float32), jnp.zeros(b_down.shape, jnp.float32))

    def step_shard(carried, inputs):
        block_tokens, block_seg, block_grad = inputs
        output, d_tokens, grads = one_shard(block_tokens, block_seg, block_grad, params)
        summed = tuple((left + right for left, right in zip(carried, grads)))
        return (summed, (output, d_tokens))
    totals, (outputs, d_all) = lax.scan(step_shard, zero_grads, (token_blocks, segment_ids, grad_blocks))
    output = outputs.reshape(N_DP * TOK_DEV, width)
    d_tokens = d_all.reshape(N_DP * TOK_DEV, width)
    return (output, d_tokens, totals[0], totals[1], totals[2], totals[3], totals[4], totals[5], totals[6], totals[7], totals[8], totals[9], totals[10], totals[11])
```

```python
import jax
import jax.numpy as jnp
from jax import lax
from jax.experimental import pallas as pl
from jax.experimental.pallas import tpu as pltpu
from jax.sharding import PartitionSpec as P

HD = 64


epsilon = 1e-05
gelu_coef = 0.7978845608028654


def gelu_value(values):
    inner = jnp.tanh(gelu_coef * (values + 0.044715 * values * values * values))
    return 0.5 * values * (1.0 + inner)


def gelu_slope(values):
    inner = jnp.tanh(gelu_coef * (values + 0.044715 * values * values * values))
    return 0.5 * (1.0 + inner) + 0.5 * values * (1.0 - inner * inner) * gelu_coef * (
        1.0 + 3.0 * 0.044715 * values * values
    )


def norm_parts(values):
    centered = values - jnp.mean(values, axis=-1, keepdims=True)
    inverse = lax.rsqrt(jnp.mean(centered * centered, axis=-1, keepdims=True) + epsilon)
    return (centered * inverse, inverse)


def norm_back(grad_in, normed, inverse, gain):
    scaled = grad_in * gain
    return inverse * (
        scaled
        - jnp.mean(scaled, axis=-1, keepdims=True)
        - normed * jnp.mean(scaled * normed, axis=-1, keepdims=True)
    )


MESH_ID = pl.DeviceIdType.MESH


def chunk_rows(start, count):
    return pl.ds(pl.multiple_of(start, count), count)


def pair_sum_kernel(part, out, from_first, sent_on, send_sem, recv_sem):
    half = part.shape[0] // 2
    count = half // 4
    me = lax.axis_index("tensor")
    col, row = me % 2, me // 2
    beside = row * 2 + (1 - col)
    across = (1 - row) * 2 + col
    far = 3 - me

    barrier = pltpu.get_barrier_semaphore()
    for peer in (beside, across):
        pl.semaphore_signal(barrier, inc=1, device_id={"tensor": peer}, device_id_type=MESH_ID)
    pl.semaphore_wait(barrier, 2)

    def upper(index):
        return chunk_rows(index * count, count)

    def lower(index):
        return chunk_rows(half + index * count, count)

    def copy(index, src, dst, peer):
        return pltpu.make_async_remote_copy(
            src_ref=src,
            dst_ref=dst,
            send_sem=send_sem.at[index],
            recv_sem=recv_sem.at[index],
            device_id={"tensor": peer},
            device_id_type=MESH_ID,
        )

    first = (
        copy(0, part.at[upper(far)], from_first.at[0], beside),
        copy(1, part.at[lower(far)], from_first.at[1], across),
        copy(2, part.at[upper(beside)], from_first.at[2], beside),
        copy(3, part.at[lower(across)], from_first.at[3], across),
    )
    for one in first:
        one.start()
    first[0].wait_recv()
    sent_on[0] = (
        part[upper(across)].astype(jnp.float32) + from_first[0].astype(jnp.float32)
    ).astype(jnp.bfloat16)
    on_upper = copy(4, sent_on.at[0], from_first.at[4], across)
    on_upper.start()
    first[1].wait_recv()
    sent_on[1] = (
        part[lower(beside)].astype(jnp.float32) + from_first[1].astype(jnp.float32)
    ).astype(jnp.bfloat16)
    on_lower = copy(5, sent_on.at[1], from_first.at[5], beside)
    on_lower.start()
    first[2].wait_recv()
    on_upper.wait_recv()
    out[upper(me)] = (
        part[upper(me)].astype(jnp.float32)
        + from_first[2].astype(jnp.float32)
        + from_first[4].astype(jnp.float32)
    ).astype(jnp.bfloat16)
    own = [
        copy(6, out.at[upper(me)], out.at[upper(me)], beside),
        copy(7, out.at[upper(me)], out.at[upper(me)], across),
    ]
    own[0].start()
    own[1].start()
    first[3].wait_recv()
    on_lower.wait_recv()
    out[lower(me)] = (
        part[lower(me)].astype(jnp.float32)
        + from_first[3].astype(jnp.float32)
        + from_first[5].astype(jnp.float32)
    ).astype(jnp.bfloat16)
    own += [
        copy(8, out.at[lower(me)], out.at[lower(me)], across),
        copy(9, out.at[lower(me)], out.at[lower(me)], beside),
    ]
    own[2].start()
    own[3].start()
    own[0].wait_recv()
    pass_upper = copy(10, out.at[upper(beside)], out.at[upper(beside)], across)
    pass_upper.start()
    own[2].wait_recv()
    pass_lower = copy(11, out.at[lower(across)], out.at[lower(across)], beside)
    pass_lower.start()
    for one in (own[1], own[3], pass_upper, pass_lower):
        one.wait_recv()
    for one in (*first, on_upper, on_lower, *own, pass_upper, pass_lower):
        one.wait_send()


def tensor_sum(part):
    rows, cols = part.shape
    if lax.axis_size("tensor") != 4 or rows % 128:
        return lax.psum(part, "tensor")
    count = rows // 8
    return pl.pallas_call(
        pair_sum_kernel,
        out_shape=jax.ShapeDtypeStruct((rows, cols), jnp.bfloat16),
        in_specs=[pl.BlockSpec(memory_space=pltpu.VMEM)],
        out_specs=pl.BlockSpec(memory_space=pltpu.VMEM),
        scratch_shapes=[
            pltpu.VMEM((6, count, cols), jnp.bfloat16),
            pltpu.VMEM((2, count, cols), jnp.bfloat16),
            pltpu.SemaphoreType.DMA((12,)),
            pltpu.SemaphoreType.DMA((12,)),
        ],
        compiler_params=pltpu.CompilerParams(
            collective_id=0, has_side_effects=True, vmem_limit_bytes=16 * 1024 * 1024
        ),
        cost_estimate=pl.CostEstimate(
            flops=0, bytes_accessed=100 * 1024 * 1024, transcendentals=0
        ),
    )(part)


def small_sum_kernel(count, mine, out, slots, send_sem, recv_sem):
    me = lax.axis_index("dp")
    barrier = pltpu.get_barrier_semaphore()
    for step in range(1, count):
        peer = (me + step) % count
        pl.semaphore_signal(barrier, inc=1, device_id={"dp": peer}, device_id_type=MESH_ID)
    pl.semaphore_wait(barrier, count - 1)
    copies = []
    for step in range(1, count):
        copies.append(
            pltpu.make_async_remote_copy(
                src_ref=mine,
                dst_ref=slots.at[me],
                send_sem=send_sem.at[step - 1],
                recv_sem=recv_sem.at[step - 1],
                device_id={"dp": (me + step) % count},
                device_id_type=MESH_ID,
            )
        )
        copies[-1].start()
    slots[me] = mine[...]
    for one in copies:
        one.wait_recv()
    total = slots[0]
    for index in range(1, count):
        total = total + slots[index]
    out[...] = total
    for one in copies:
        one.wait_send()


def small_sum(values):
    count = lax.axis_size("dp")
    shape = values.shape
    flat = values.reshape(-1, 128)
    total = pl.pallas_call(
        lambda *refs: small_sum_kernel(count, *refs),
        out_shape=jax.ShapeDtypeStruct(flat.shape, jnp.float32),
        in_specs=[pl.BlockSpec(memory_space=pltpu.VMEM)],
        out_specs=pl.BlockSpec(memory_space=pltpu.VMEM),
        scratch_shapes=[
            pltpu.VMEM((count,) + flat.shape, jnp.float32),
            pltpu.SemaphoreType.DMA((count - 1,)),
            pltpu.SemaphoreType.DMA((count - 1,)),
        ],
        compiler_params=pltpu.CompilerParams(
            collective_id=1, has_side_effects=True, vmem_limit_bytes=4 * 1024 * 1024
        ),
    )(flat)
    return total.reshape(shape)


def block_mask(seg_query, seg_keys, first_row):
    shape_here = (seg_query.shape[0], seg_keys.shape[0])
    query_pos = first_row + lax.broadcasted_iota(jnp.int32, shape_here, 0)
    key_pos = lax.broadcasted_iota(jnp.int32, shape_here, 1)
    return (seg_query[:, None] == seg_keys[None, :]) & (key_pos <= query_pos)


def attention_forward(query_heads, key_heads, value_heads, seg_row):
    length = query_heads.shape[1]
    block_rows = 512
    scale = query_heads.shape[2] ** (-0.5)
    outputs = []
    totals = []
    for first_row in range(0, length, block_rows):
        rows_q = query_heads[:, first_row : first_row + block_rows]
        scores = (
            jnp.einsum("hqd,hkd->hqk", rows_q, key_heads, preferred_element_type=jnp.float32)
            * scale
        )
        allowed = block_mask(seg_row[first_row : first_row + block_rows], seg_row, first_row)
        scores = jnp.where(allowed[None], scores, -jnp.inf)
        maximum = jnp.max(scores, axis=-1, keepdims=True)
        log_total = jnp.log(jnp.sum(jnp.exp(scores - maximum), axis=-1, keepdims=True)) + maximum
        weights_bf = jnp.exp(scores - log_total).astype(jnp.bfloat16)
        outputs.append(
            jnp.einsum(
                "hqk,hkd->hqd", weights_bf, value_heads, preferred_element_type=jnp.float32
            ).astype(jnp.bfloat16)
        )
        totals.append(log_total)
    return (jnp.concatenate(outputs, axis=1), jnp.concatenate(totals, axis=1))


def attention_backward(query_heads, key_heads, value_heads, seg_row, log_totals, grad_ctx):
    length = query_heads.shape[1]
    block_rows = 512
    scale = query_heads.shape[2] ** (-0.5)
    grad_keys = jnp.zeros(key_heads.shape, jnp.float32)
    grad_values = jnp.zeros(value_heads.shape, jnp.float32)
    grad_queries = []
    for first_row in range(0, length, block_rows):
        rows_q = query_heads[:, first_row : first_row + block_rows]
        scores = (
            jnp.einsum("hqd,hkd->hqk", rows_q, key_heads, preferred_element_type=jnp.float32)
            * scale
        )
        allowed = block_mask(seg_row[first_row : first_row + block_rows], seg_row, first_row)
        scores = jnp.where(allowed[None], scores, -jnp.inf)
        weights = jnp.exp(scores - log_totals[:, first_row : first_row + block_rows])
        weights_bf = weights.astype(jnp.bfloat16)
        grad_rows_ctx = grad_ctx[:, first_row : first_row + block_rows]
        grad_weights = jnp.einsum(
            "hqd,hkd->hqk", grad_rows_ctx, value_heads, preferred_element_type=jnp.float32
        )
        inner_sum = jnp.sum(weights * grad_weights, axis=-1, keepdims=True)
        grad_scores = (weights * (grad_weights - inner_sum)).astype(jnp.bfloat16)
        grad_queries.append(
            (
                jnp.einsum(
                    "hqk,hkd->hqd", grad_scores, key_heads, preferred_element_type=jnp.float32
                )
                * scale
            ).astype(jnp.bfloat16)
        )
        grad_keys = (
            grad_keys
            + jnp.einsum("hqk,hqd->hkd", grad_scores, rows_q, preferred_element_type=jnp.float32)
            * scale
        )
        grad_values = grad_values + jnp.einsum(
            "hqk,hqd->hkd", weights_bf, grad_rows_ctx, preferred_element_type=jnp.float32
        )
    return (
        jnp.concatenate(grad_queries, axis=1),
        grad_keys.astype(jnp.bfloat16),
        grad_values.astype(jnp.bfloat16),
    )


def per_device(
    tokens,
    segment_ids,
    ln1_gain,
    ln1_shift,
    w_qkv,
    b_qv,
    w_out,
    b_out,
    ln2_gain,
    ln2_shift,
    w_up,
    b_up,
    w_down,
    b_down,
    d_out,
):
    seg_row = segment_ids[0]
    length = tokens.shape[0]
    local_width = w_qkv.shape[2]
    head_count = local_width // HD
    tokens_f = tokens.astype(jnp.float32)
    normed1, inverse1 = norm_parts(tokens_f)
    input1 = (normed1 * ln1_gain + ln1_shift).astype(jnp.bfloat16)
    projected = jnp.einsum("sd,ide->ise", input1, w_qkv, preferred_element_type=jnp.float32)
    bias_rows = jnp.stack([b_qv[0], jnp.zeros_like(b_qv[0]), b_qv[1]])
    projected = (projected + bias_rows[:, None, :]).astype(jnp.bfloat16)
    split_heads = projected.reshape(3, length, head_count, HD).transpose(0, 2, 1, 3)
    query_heads, key_heads, value_heads = (split_heads[0], split_heads[1], split_heads[2])
    context_heads, log_totals = attention_forward(query_heads, key_heads, value_heads, seg_row)
    context = context_heads.transpose(1, 0, 2).reshape(length, local_width)
    attn_part = jnp.dot(context, w_out, preferred_element_type=jnp.float32)
    attn_sum = tensor_sum(attn_part.astype(jnp.bfloat16)).astype(jnp.float32)
    resid_mid = tokens_f + attn_sum + b_out
    normed2, inverse2 = norm_parts(resid_mid)
    input2 = (normed2 * ln2_gain + ln2_shift).astype(jnp.bfloat16)
    pre_act = jnp.dot(input2, w_up, preferred_element_type=jnp.float32) + b_up
    activated = gelu_value(pre_act).astype(jnp.bfloat16)
    mlp_part = jnp.dot(activated, w_down, preferred_element_type=jnp.float32).astype(jnp.bfloat16)
    grad_out = d_out.astype(jnp.float32)
    g_down_bias = jnp.sum(grad_out, axis=0)
    grad_act = jnp.einsum("sd,fd->sf", d_out, w_down, preferred_element_type=jnp.float32)
    grad_pre = (grad_act * gelu_slope(pre_act)).astype(jnp.bfloat16)
    g_up_bias = jnp.sum(grad_pre.astype(jnp.float32), axis=0)
    normed_part = jnp.einsum(
        "sf,df->sd", grad_pre, w_up, preferred_element_type=jnp.float32
    ).astype(jnp.bfloat16)
    g_down = jnp.einsum("sf,sd->fd", activated, d_out, preferred_element_type=jnp.float32).astype(
        jnp.bfloat16
    )
    g_up = jnp.einsum("sd,sf->df", input2, grad_pre, preferred_element_type=jnp.float32).astype(
        jnp.bfloat16
    )
    g_down, g_up, normed_part, mlp_part = lax.optimization_barrier(
        (g_down, g_up, normed_part, mlp_part)
    )
    g_down, g_up = lax.psum((g_down, g_up), "dp")
    normed_grad = tensor_sum(normed_part).astype(jnp.float32)
    mlp_sum = tensor_sum(mlp_part).astype(jnp.float32)
    output = (resid_mid + mlp_sum + b_down).astype(jnp.bfloat16)
    resid_grad = grad_out + norm_back(normed_grad, normed2, inverse2, ln2_gain)
    g_ln2_gain = jnp.sum(normed_grad * normed2, axis=0)
    g_ln2_shift = jnp.sum(normed_grad, axis=0)
    g_out_bias = jnp.sum(resid_grad, axis=0)
    resid_grad_bf = resid_grad.astype(jnp.bfloat16)
    g_out = jnp.einsum("sk,sd->kd", context, resid_grad_bf, preferred_element_type=jnp.float32)
    grad_context = jnp.einsum(
        "sd,kd->sk", resid_grad_bf, w_out, preferred_element_type=jnp.float32
    ).astype(jnp.bfloat16)
    grad_ctx_heads = grad_context.reshape(length, head_count, HD).transpose(1, 0, 2)
    grad_q, grad_k, grad_v = attention_backward(
        query_heads, key_heads, value_heads, seg_row, log_totals, grad_ctx_heads
    )
    grad_proj = (
        jnp.stack([grad_q, grad_k, grad_v]).transpose(0, 2, 1, 3).reshape(3, length, local_width)
    )
    g_qkv = jnp.einsum(
        "sd,ise->ide", input1, grad_proj, preferred_element_type=jnp.float32
    ).astype(jnp.bfloat16)
    g_qv_bias = jnp.concatenate(
        [
            jnp.sum(grad_proj[0].astype(jnp.float32), axis=0),
            jnp.sum(grad_proj[2].astype(jnp.float32), axis=0),
        ]
    )
    input_part = jnp.einsum(
        "ise,ide->sd", grad_proj, w_qkv, preferred_element_type=jnp.float32
    ).astype(jnp.bfloat16)
    width = tokens.shape[1]
    small_parts = [g_up_bias.reshape(-1), g_qv_bias, g_out_bias, g_ln2_gain, g_ln2_shift, g_down_bias]
    sizes = [one.shape[0] for one in small_parts]
    flat = jnp.concatenate(small_parts)
    small_rows = -(-flat.shape[0] // width)
    small_rows = -(-small_rows // 16) * 16
    flat = jnp.pad(flat, (0, small_rows * width - flat.shape[0])).reshape(small_rows, width)
    g_out_all = jnp.concatenate([g_out, flat], axis=0).astype(jnp.bfloat16)
    g_qkv, g_out_all, input_part, g_down, g_up = lax.optimization_barrier(
        (g_qkv, g_out_all, input_part, g_down, g_up)
    )
    g_qkv, g_out_all = lax.psum((g_qkv, g_out_all), "dp")
    input_grad = tensor_sum(input_part).astype(jnp.float32)
    d_tokens = (resid_grad + norm_back(input_grad, normed1, inverse1, ln1_gain)).astype(
        jnp.bfloat16
    )
    ln1_pair = small_sum(
        jnp.stack([jnp.sum(input_grad * normed1, axis=0), jnp.sum(input_grad, axis=0)])
    )
    g_ln1_gain, g_ln1_shift = ln1_pair[0], ln1_pair[1]
    g_down = g_down.astype(jnp.float32)
    g_up = g_up.astype(jnp.float32)
    g_qkv = g_qkv.astype(jnp.float32)
    g_out_all = g_out_all.astype(jnp.float32)
    g_out = g_out_all[:local_width]
    small_all = g_out_all[local_width:].reshape(-1)
    pieces = []
    begin = 0
    for size in sizes:
        pieces.append(small_all[begin : begin + size])
        begin += size
    g_up_bias, g_qv_bias, g_out_bias, g_ln2_gain, g_ln2_shift, g_down_bias = pieces
    g_qv_bias = g_qv_bias.reshape(2, local_width)
    return (
        output,
        d_tokens,
        g_ln1_gain,
        g_ln1_shift,
        g_qkv,
        g_qv_bias,
        g_out,
        g_out_bias,
        g_ln2_gain,
        g_ln2_shift,
        g_up,
        g_up_bias,
        g_down,
        g_down_bias,
    )


def solution(mesh):
    placed = (
        P("dp", None),
        P("dp", None),
        P(),
        P(),
        P(None, None, "tensor"),
        P(None, "tensor"),
        P("tensor", None),
        P(),
        P(),
        P(),
        P(None, "tensor"),
        P("tensor"),
        P("tensor", None),
        P(),
        P("dp", None),
    )
    return jax.shard_map(
        per_device,
        mesh=mesh,
        in_specs=placed,
        out_specs=(
            P("dp", None),
            P("dp", None),
            P(),
            P(),
            P(None, None, "tensor"),
            P(None, "tensor"),
            P("tensor", None),
            P(),
            P(),
            P(),
            P(None, "tensor"),
            P("tensor"),
            P("tensor", None),
            P(),
        ),
        check_vma=False,
    )
```

```python
import jax
import jax.numpy as jnp
from jax import lax
from jax.experimental import pallas as pl
from jax.experimental.pallas import tpu as pltpu
from jax.sharding import PartitionSpec as P

HD = 64


epsilon = 1e-05
gelu_coef = 0.7978845608028654


def gelu_value(values):
    inner = jnp.tanh(gelu_coef * (values + 0.044715 * values * values * values))
    return 0.5 * values * (1.0 + inner)


def gelu_slope(values):
    inner = jnp.tanh(gelu_coef * (values + 0.044715 * values * values * values))
    return 0.5 * (1.0 + inner) + 0.5 * values * (1.0 - inner * inner) * gelu_coef * (
        1.0 + 3.0 * 0.044715 * values * values
    )


def norm_parts(values):
    centered = values - jnp.mean(values, axis=-1, keepdims=True)
    inverse = lax.rsqrt(jnp.mean(centered * centered, axis=-1, keepdims=True) + epsilon)
    return (centered * inverse, inverse)


def norm_back(grad_in, normed, inverse, gain):
    scaled = grad_in * gain
    return inverse * (
        scaled
        - jnp.mean(scaled, axis=-1, keepdims=True)
        - normed * jnp.mean(scaled * normed, axis=-1, keepdims=True)
    )


MESH_ID = pl.DeviceIdType.MESH


def chunk_rows(start, count):
    return pl.ds(pl.multiple_of(start, count), count)


def pair_sum_kernel(part, out, from_first, sent_on, send_sem, recv_sem):
    half = part.shape[0] // 2
    count = half // 4
    me = lax.axis_index("tensor")
    col, row = me % 2, me // 2
    beside = row * 2 + (1 - col)
    across = (1 - row) * 2 + col
    far = 3 - me

    barrier = pltpu.get_barrier_semaphore()
    for peer in (beside, across):
        pl.semaphore_signal(barrier, inc=1, device_id={"tensor": peer}, device_id_type=MESH_ID)
    pl.semaphore_wait(barrier, 2)

    def upper(index):
        return chunk_rows(index * count, count)

    def lower(index):
        return chunk_rows(half + index * count, count)

    def copy(index, src, dst, peer):
        return pltpu.make_async_remote_copy(
            src_ref=src,
            dst_ref=dst,
            send_sem=send_sem.at[index],
            recv_sem=recv_sem.at[index],
            device_id={"tensor": peer},
            device_id_type=MESH_ID,
        )

    first = (
        copy(0, part.at[upper(far)], from_first.at[0], beside),
        copy(1, part.at[lower(far)], from_first.at[1], across),
        copy(2, part.at[upper(beside)], from_first.at[2], beside),
        copy(3, part.at[lower(across)], from_first.at[3], across),
    )
    for one in first:
        one.start()
    first[0].wait_recv()
    sent_on[0] = (
        part[upper(across)].astype(jnp.float32) + from_first[0].astype(jnp.float32)
    ).astype(jnp.bfloat16)
    on_upper = copy(4, sent_on.at[0], from_first.at[4], across)
    on_upper.start()
    first[1].wait_recv()
    sent_on[1] = (
        part[lower(beside)].astype(jnp.float32) + from_first[1].astype(jnp.float32)
    ).astype(jnp.bfloat16)
    on_lower = copy(5, sent_on.at[1], from_first.at[5], beside)
    on_lower.start()
    first[2].wait_recv()
    on_upper.wait_recv()
    out[upper(me)] = (
        part[upper(me)].astype(jnp.float32)
        + from_first[2].astype(jnp.float32)
        + from_first[4].astype(jnp.float32)
    ).astype(jnp.bfloat16)
    own = [
        copy(6, out.at[upper(me)], out.at[upper(me)], beside),
        copy(7, out.at[upper(me)], out.at[upper(me)], across),
    ]
    own[0].start()
    own[1].start()
    first[3].wait_recv()
    on_lower.wait_recv()
    out[lower(me)] = (
        part[lower(me)].astype(jnp.float32)
        + from_first[3].astype(jnp.float32)
        + from_first[5].astype(jnp.float32)
    ).astype(jnp.bfloat16)
    own += [
        copy(8, out.at[lower(me)], out.at[lower(me)], across),
        copy(9, out.at[lower(me)], out.at[lower(me)], beside),
    ]
    own[2].start()
    own[3].start()
    own[0].wait_recv()
    pass_upper = copy(10, out.at[upper(beside)], out.at[upper(beside)], across)
    pass_upper.start()
    own[2].wait_recv()
    pass_lower = copy(11, out.at[lower(across)], out.at[lower(across)], beside)
    pass_lower.start()
    for one in (own[1], own[3], pass_upper, pass_lower):
        one.wait_recv()
    for one in (*first, on_upper, on_lower, *own, pass_upper, pass_lower):
        one.wait_send()


def core_groups():
    count = lax.axis_size("dp")
    pairs = [[index, index + 1] for index in range(0, count, 2)]
    return pairs, [list(range(side, count, 2)) for side in range(2)]


def pair_scatter(values):
    return lax.psum_scatter(
        values, "dp", scatter_dimension=0, axis_index_groups=core_groups()[0], tiled=True
    )


def finish_sum(half):
    pairs, sides = core_groups()
    half = lax.psum(half, "dp", axis_index_groups=sides)
    return lax.all_gather(half, "dp", axis=0, axis_index_groups=pairs, tiled=True)


def tensor_sum(part):
    rows, cols = part.shape
    if lax.axis_size("tensor") != 4 or rows % 128:
        return lax.psum(part, "tensor")
    count = rows // 8
    return pl.pallas_call(
        pair_sum_kernel,
        out_shape=jax.ShapeDtypeStruct((rows, cols), jnp.bfloat16),
        in_specs=[pl.BlockSpec(memory_space=pltpu.VMEM)],
        out_specs=pl.BlockSpec(memory_space=pltpu.VMEM),
        scratch_shapes=[
            pltpu.VMEM((6, count, cols), jnp.bfloat16),
            pltpu.VMEM((2, count, cols), jnp.bfloat16),
            pltpu.SemaphoreType.DMA((12,)),
            pltpu.SemaphoreType.DMA((12,)),
        ],
        compiler_params=pltpu.CompilerParams(
            collective_id=0, has_side_effects=True, vmem_limit_bytes=16 * 1024 * 1024
        ),
        cost_estimate=pl.CostEstimate(
            flops=0, bytes_accessed=100 * 1024 * 1024, transcendentals=0
        ),
    )(part)


def small_sum_kernel(count, mine, out, slots, send_sem, recv_sem):
    me = lax.axis_index("dp")
    barrier = pltpu.get_barrier_semaphore()
    for step in range(1, count):
        peer = (me + step) % count
        pl.semaphore_signal(barrier, inc=1, device_id={"dp": peer}, device_id_type=MESH_ID)
    pl.semaphore_wait(barrier, count - 1)
    copies = []
    for step in range(1, count):
        copies.append(
            pltpu.make_async_remote_copy(
                src_ref=mine,
                dst_ref=slots.at[me],
                send_sem=send_sem.at[step - 1],
                recv_sem=recv_sem.at[step - 1],
                device_id={"dp": (me + step) % count},
                device_id_type=MESH_ID,
            )
        )
        copies[-1].start()
    slots[me] = mine[...]
    for one in copies:
        one.wait_recv()
    total = slots[0]
    for index in range(1, count):
        total = total + slots[index]
    out[...] = total
    for one in copies:
        one.wait_send()


def small_sum(values):
    count = lax.axis_size("dp")
    shape = values.shape
    flat = values.reshape(-1, 128)
    total = pl.pallas_call(
        lambda *refs: small_sum_kernel(count, *refs),
        out_shape=jax.ShapeDtypeStruct(flat.shape, jnp.float32),
        in_specs=[pl.BlockSpec(memory_space=pltpu.VMEM)],
        out_specs=pl.BlockSpec(memory_space=pltpu.VMEM),
        scratch_shapes=[
            pltpu.VMEM((count,) + flat.shape, jnp.float32),
            pltpu.SemaphoreType.DMA((count - 1,)),
            pltpu.SemaphoreType.DMA((count - 1,)),
        ],
        compiler_params=pltpu.CompilerParams(
            collective_id=1, has_side_effects=True, vmem_limit_bytes=4 * 1024 * 1024
        ),
    )(flat)
    return total.reshape(shape)


def block_mask(seg_query, seg_keys, first_row):
    shape_here = (seg_query.shape[0], seg_keys.shape[0])
    query_pos = first_row + lax.broadcasted_iota(jnp.int32, shape_here, 0)
    key_pos = lax.broadcasted_iota(jnp.int32, shape_here, 1)
    return (seg_query[:, None] == seg_keys[None, :]) & (key_pos <= query_pos)


def attention_forward(query_heads, key_heads, value_heads, seg_row):
    length = query_heads.shape[1]
    block_rows = 512
    scale = query_heads.shape[2] ** (-0.5)
    outputs = []
    totals = []
    for first_row in range(0, length, block_rows):
        rows_q = query_heads[:, first_row : first_row + block_rows]
        scores = (
            jnp.einsum("hqd,hkd->hqk", rows_q, key_heads, preferred_element_type=jnp.float32)
            * scale
        )
        allowed = block_mask(seg_row[first_row : first_row + block_rows], seg_row, first_row)
        scores = jnp.where(allowed[None], scores, -jnp.inf)
        maximum = jnp.max(scores, axis=-1, keepdims=True)
        log_total = jnp.log(jnp.sum(jnp.exp(scores - maximum), axis=-1, keepdims=True)) + maximum
        weights_bf = jnp.exp(scores - log_total).astype(jnp.bfloat16)
        outputs.append(
            jnp.einsum(
                "hqk,hkd->hqd", weights_bf, value_heads, preferred_element_type=jnp.float32
            ).astype(jnp.bfloat16)
        )
        totals.append(log_total)
    return (jnp.concatenate(outputs, axis=1), jnp.concatenate(totals, axis=1))


def attention_backward(query_heads, key_heads, value_heads, seg_row, log_totals, grad_ctx):
    length = query_heads.shape[1]
    block_rows = 512
    scale = query_heads.shape[2] ** (-0.5)
    grad_keys = jnp.zeros(key_heads.shape, jnp.float32)
    grad_values = jnp.zeros(value_heads.shape, jnp.float32)
    grad_queries = []
    for first_row in range(0, length, block_rows):
        rows_q = query_heads[:, first_row : first_row + block_rows]
        scores = (
            jnp.einsum("hqd,hkd->hqk", rows_q, key_heads, preferred_element_type=jnp.float32)
            * scale
        )
        allowed = block_mask(seg_row[first_row : first_row + block_rows], seg_row, first_row)
        scores = jnp.where(allowed[None], scores, -jnp.inf)
        weights = jnp.exp(scores - log_totals[:, first_row : first_row + block_rows])
        weights_bf = weights.astype(jnp.bfloat16)
        grad_rows_ctx = grad_ctx[:, first_row : first_row + block_rows]
        grad_weights = jnp.einsum(
            "hqd,hkd->hqk", grad_rows_ctx, value_heads, preferred_element_type=jnp.float32
        )
        inner_sum = jnp.sum(weights * grad_weights, axis=-1, keepdims=True)
        grad_scores = (weights * (grad_weights - inner_sum)).astype(jnp.bfloat16)
        grad_queries.append(
            (
                jnp.einsum(
                    "hqk,hkd->hqd", grad_scores, key_heads, preferred_element_type=jnp.float32
                )
                * scale
            ).astype(jnp.bfloat16)
        )
        grad_keys = (
            grad_keys
            + jnp.einsum("hqk,hqd->hkd", grad_scores, rows_q, preferred_element_type=jnp.float32)
            * scale
        )
        grad_values = grad_values + jnp.einsum(
            "hqk,hqd->hkd", weights_bf, grad_rows_ctx, preferred_element_type=jnp.float32
        )
    return (
        jnp.concatenate(grad_queries, axis=1),
        grad_keys.astype(jnp.bfloat16),
        grad_values.astype(jnp.bfloat16),
    )


def per_device(
    tokens,
    segment_ids,
    ln1_gain,
    ln1_shift,
    w_qkv,
    b_qv,
    w_out,
    b_out,
    ln2_gain,
    ln2_shift,
    w_up,
    b_up,
    w_down,
    b_down,
    d_out,
):
    seg_row = segment_ids[0]
    length = tokens.shape[0]
    local_width = w_qkv.shape[2]
    head_count = local_width // HD
    tokens_f = tokens.astype(jnp.float32)
    normed1, inverse1 = norm_parts(tokens_f)
    input1 = (normed1 * ln1_gain + ln1_shift).astype(jnp.bfloat16)
    projected = jnp.einsum("sd,ide->ise", input1, w_qkv, preferred_element_type=jnp.float32)
    bias_rows = jnp.stack([b_qv[0], jnp.zeros_like(b_qv[0]), b_qv[1]])
    projected = (projected + bias_rows[:, None, :]).astype(jnp.bfloat16)
    split_heads = projected.reshape(3, length, head_count, HD).transpose(0, 2, 1, 3)
    query_heads, key_heads, value_heads = (split_heads[0], split_heads[1], split_heads[2])
    context_heads, log_totals = attention_forward(query_heads, key_heads, value_heads, seg_row)
    context = context_heads.transpose(1, 0, 2).reshape(length, local_width)
    attn_part = jnp.dot(context, w_out, preferred_element_type=jnp.float32)
    attn_sum = tensor_sum(attn_part.astype(jnp.bfloat16)).astype(jnp.float32)
    resid_mid = tokens_f + attn_sum + b_out
    normed2, inverse2 = norm_parts(resid_mid)
    input2 = (normed2 * ln2_gain + ln2_shift).astype(jnp.bfloat16)
    pre_act = jnp.dot(input2, w_up, preferred_element_type=jnp.float32) + b_up
    activated = gelu_value(pre_act).astype(jnp.bfloat16)
    mlp_part = jnp.dot(activated, w_down, preferred_element_type=jnp.float32).astype(jnp.bfloat16)
    grad_out = d_out.astype(jnp.float32)
    g_down_bias = jnp.sum(grad_out, axis=0)
    grad_act = jnp.einsum("sd,fd->sf", d_out, w_down, preferred_element_type=jnp.float32)
    grad_pre = (grad_act * gelu_slope(pre_act)).astype(jnp.bfloat16)
    g_up_bias = jnp.sum(grad_pre.astype(jnp.float32), axis=0)
    normed_part = jnp.einsum(
        "sf,df->sd", grad_pre, w_up, preferred_element_type=jnp.float32
    ).astype(jnp.bfloat16)
    g_down = jnp.einsum("sf,sd->fd", activated, d_out, preferred_element_type=jnp.float32).astype(
        jnp.bfloat16
    )
    g_up = jnp.einsum("sd,sf->df", input2, grad_pre, preferred_element_type=jnp.float32).astype(
        jnp.bfloat16
    )
    g_down, g_up, normed_part, mlp_part = lax.optimization_barrier(
        (g_down, g_up, normed_part, mlp_part)
    )
    width = tokens.shape[1]
    down_up_half = pair_scatter(jnp.concatenate([g_down, g_up.reshape(-1, width)], axis=0))
    down_up_half, normed_sum = lax.optimization_barrier((down_up_half, tensor_sum(normed_part)))
    g_down_up = finish_sum(down_up_half)
    mlp_part, normed_sum = lax.optimization_barrier((mlp_part, normed_sum))
    normed_grad = normed_sum.astype(jnp.float32)
    mlp_sum = tensor_sum(mlp_part).astype(jnp.float32)
    output = (resid_mid + mlp_sum + b_down).astype(jnp.bfloat16)
    resid_grad = grad_out + norm_back(normed_grad, normed2, inverse2, ln2_gain)
    g_ln2_gain = jnp.sum(normed_grad * normed2, axis=0)
    g_ln2_shift = jnp.sum(normed_grad, axis=0)
    g_out_bias = jnp.sum(resid_grad, axis=0)
    resid_grad_bf = resid_grad.astype(jnp.bfloat16)
    g_out = jnp.einsum("sk,sd->kd", context, resid_grad_bf, preferred_element_type=jnp.float32)
    grad_context = jnp.einsum(
        "sd,kd->sk", resid_grad_bf, w_out, preferred_element_type=jnp.float32
    ).astype(jnp.bfloat16)
    small_parts = [g_up_bias.reshape(-1), g_out_bias, g_ln2_gain, g_ln2_shift, g_down_bias]
    sizes = [one.shape[0] for one in small_parts]
    flat = jnp.concatenate(small_parts)
    small_rows = -(-flat.shape[0] // width)
    small_rows = -(-small_rows // 16) * 16
    flat = jnp.pad(flat, (0, small_rows * width - flat.shape[0])).reshape(small_rows, width)
    g_out_all = jnp.concatenate([g_out, flat], axis=0).astype(jnp.bfloat16)
    g_out_all, grad_context = lax.optimization_barrier((g_out_all, grad_context))
    g_out_all = lax.psum(g_out_all, "dp")
    grad_ctx_heads = grad_context.reshape(length, head_count, HD).transpose(1, 0, 2)
    grad_q, grad_k, grad_v = attention_backward(
        query_heads, key_heads, value_heads, seg_row, log_totals, grad_ctx_heads
    )
    grad_proj = (
        jnp.stack([grad_q, grad_k, grad_v]).transpose(0, 2, 1, 3).reshape(3, length, local_width)
    )
    g_qkv = jnp.einsum(
        "sd,ise->ide", input1, grad_proj, preferred_element_type=jnp.float32
    ).astype(jnp.bfloat16)
    g_qv_bias = jnp.concatenate(
        [
            jnp.sum(grad_proj[0].astype(jnp.float32), axis=0),
            jnp.sum(grad_proj[2].astype(jnp.float32), axis=0),
        ]
    )
    input_part = jnp.einsum(
        "ise,ide->sd", grad_proj, w_qkv, preferred_element_type=jnp.float32
    ).astype(jnp.bfloat16)
    width = tokens.shape[1]
    g_qkv, input_part, g_down_up = lax.optimization_barrier((g_qkv, input_part, g_down_up))
    qkv_half = pair_scatter(g_qkv.reshape(-1, local_width))
    qkv_half, input_sum = lax.optimization_barrier((qkv_half, tensor_sum(input_part)))
    g_qkv = finish_sum(qkv_half).reshape(g_qkv.shape)
    input_grad = input_sum.astype(jnp.float32)
    d_tokens = (resid_grad + norm_back(input_grad, normed1, inverse1, ln1_gain)).astype(
        jnp.bfloat16
    )
    last = small_sum(
        jnp.concatenate(
            [jnp.sum(input_grad * normed1, axis=0), jnp.sum(input_grad, axis=0), g_qv_bias]
        )
    )
    g_ln1_gain, g_ln1_shift = last[:width], last[width : 2 * width]
    g_qv_bias = last[2 * width :].reshape(2, local_width)
    hidden = w_down.shape[0]
    g_down = g_down_up[:hidden].astype(jnp.float32)
    g_up = g_down_up[hidden:].reshape(width, hidden).astype(jnp.float32)
    g_qkv = g_qkv.astype(jnp.float32)
    g_out_all = g_out_all.astype(jnp.float32)
    g_out = g_out_all[:local_width]
    small_all = g_out_all[local_width:].reshape(-1)
    pieces = []
    begin = 0
    for size in sizes:
        pieces.append(small_all[begin : begin + size])
        begin += size
    g_up_bias, g_out_bias, g_ln2_gain, g_ln2_shift, g_down_bias = pieces
    return (
        output,
        d_tokens,
        g_ln1_gain,
        g_ln1_shift,
        g_qkv,
        g_qv_bias,
        g_out,
        g_out_bias,
        g_ln2_gain,
        g_ln2_shift,
        g_up,
        g_up_bias,
        g_down,
        g_down_bias,
    )


def solution(mesh):
    placed = (
        P("dp", None),
        P("dp", None),
        P(),
        P(),
        P(None, None, "tensor"),
        P(None, "tensor"),
        P("tensor", None),
        P(),
        P(),
        P(),
        P(None, "tensor"),
        P("tensor"),
        P("tensor", None),
        P(),
        P("dp", None),
    )
    return jax.shard_map(
        per_device,
        mesh=mesh,
        in_specs=placed,
        out_specs=(
            P("dp", None),
            P("dp", None),
            P(),
            P(),
            P(None, None, "tensor"),
            P(None, "tensor"),
            P("tensor", None),
            P(),
            P(),
            P(),
            P(None, "tensor"),
            P("tensor"),
            P("tensor", None),
            P(),
        ),
        check_vma=False,
    )
```
